32 devices in a mesh: ctx: 16 (over z, x, core), tp: 2 (over y).
Axes of the slice: x: 2, y: 2, z: 4, core: 2. Of those that a mesh axis runs over, the one named last changes fastest.
Arguments:
- hidden: bfloat16 [2048, 7168], P('ctx', 'tp'), may hold values from -500 to 500
- embed: bfloat16 [2048, 7168], P('ctx', 'tp'), may hold values from -500 to 500
- gain_hidden: float32 [7168], P('tp'), may hold values from 0.1 to 1.9
- gain_embed: float32 [7168], P('tp'), may hold values from 0.1 to 1.9
- proj_hidden: bfloat16 [7168, 576], P('tp'), may hold values from -0.0625 to 0.0625
- proj_embed: bfloat16 [7168, 576], P('tp'), may hold values from -0.0625 to 0.0625
- gain_latent: float32 [512], replicated, may hold values from 0.1 to 1.9
- key_up: bfloat16 [512, 8192], P(None, 'tp'), may hold values from -0.25 to 0.25
- value_up: bfloat16 [512, 8192], P(None, 'tp'), may hold values from -0.25 to 0.25
- queries: bfloat16 [2048, 12288], P('ctx', 'tp'), may hold values from -60 to 60
- grad_out: bfloat16 [2048, 8192], P('ctx', 'tp'), may hold values from -6 to 6
Outputs:
- attended: bfloat16 [2048, 8192], P('ctx', 'tp')
- grad_queries: bfloat16 [2048, 12288], P('ctx', 'tp')
- grad_hidden: bfloat16 [2048, 7168], P('ctx', 'tp')
- grad_embed: bfloat16 [2048, 7168], P('ctx', 'tp')
The draws below stay inside these ranges and needn't reach their ends.
All inputs are finite; a program needn't handle non-finite values.
Results may differ from the reference program's by a relative error of at most 0.019.
The reference program's roundings to bfloat16 on the way count: a program that leaves them out, or rounds other values in their place, can miss the bound.
Values may be sent and summed in bfloat16 or wider, within the bound.
A program may use at most 192 MiB of HBM per device.

```python
import math
import jax
import jax.numpy as jnp
from jax import lax

D = 7168
LAT = 512
ROPE = 64
NOPE = 128
VDIM = 128
H = 64
SEQ = 2048
N_CTX = 16


def feature_values(key, row_count, column_count):
    splits = jax.random.split(key, 3)
    column_ramp = jnp.arange(column_count, dtype=jnp.float32) / column_count
    base_values = jnp.clip(jax.random.normal(splits[0], (row_count, column_count), jnp.float32), -6.0, 6.0)
    row_scale = jnp.exp(jax.random.uniform(splits[1], (row_count, 1), jnp.float32, 0.0, math.log(10.0)))
    column_scale = 3.0 ** column_ramp * jnp.exp(jax.random.uniform(splits[2], (column_count,), jnp.float32, 0.0, math.log(3.4)))
    return base_values * row_scale * column_scale / 3.0


def draw_hidden(key, part):
    return feature_values(jax.random.fold_in(key, 101), SEQ, D).astype(jnp.bfloat16)


def draw_embed(key, part):
    return feature_values(jax.random.fold_in(key, 202), SEQ, D).astype(jnp.bfloat16)


def draw_queries(key, part):
    splits = jax.random.split(jax.random.fold_in(key, 303), 1)
    array_shape = (SEQ, H * (NOPE + ROPE))
    values = 2.5 * jnp.clip(jax.random.normal(splits[0], array_shape, jnp.float32), -6.0, 6.0)
    return values.astype(jnp.bfloat16)


def shard_levels(own_key, extent, cuts, low, top_value):
    def one(axis_at, blocks):
        heights = jax.random.uniform(jax.random.fold_in(jax.random.fold_in(own_key, 6), axis_at), (blocks,), jnp.float32, low / len(cuts), top_value / len(cuts))
        return jnp.repeat(jnp.exp(heights), extent[axis_at] // blocks).reshape((-1,) + (1,) * (len(extent) - axis_at - 1))

    level = one(*cuts[0])
    for cut in cuts[1:]:
        level = level * one(*cut)
    return level


def centred(key, extent, spread, limit, cuts=(), kind=jnp.bfloat16):
    values = jax.random.normal(key, extent, jnp.float32) * spread
    if len(cuts) > 0:
        values = shard_levels(key, extent, cuts, -0.22, 0.18) * values
    return jnp.clip(values, min=-limit, max=limit).astype(kind)


def setup_inputs(seed: int = 0) -> dict:
    seeds = jax.random.split(jax.random.key(seed), 12)
    return {
        "hidden": draw_hidden(jax.random.fold_in(seeds[11], 71), 0),
        "embed": draw_embed(jax.random.fold_in(seeds[11], 71), 0),
        "gain_hidden": jnp.clip(1.0 + 0.18 * jax.random.normal(seeds[2], (D,), jnp.float32), 0.1, 1.9),
        "gain_embed": jnp.clip(1.0 + 0.18 * jax.random.normal(seeds[3], (D,), jnp.float32), 0.1, 1.9),
        "proj_hidden": centred(seeds[4], (D, LAT + ROPE), D ** -0.5, 0.0625, ((0, 2),)),
        "proj_embed": centred(seeds[5], (D, LAT + ROPE), D ** -0.5, 0.0625, ((0, 2),)),
        "gain_latent": jnp.clip(1.0 + 0.18 * jax.random.normal(seeds[6], (LAT,), jnp.float32), 0.1, 1.9),
        "key_up": centred(seeds[7], (LAT, H * NOPE), LAT ** -0.5, 0.25, ((1, 2),)),
        "value_up": centred(seeds[8], (LAT, H * VDIM), LAT ** -0.5, 0.25, ((1, 2),)),
        "queries": draw_queries(jax.random.fold_in(seeds[11], 71), 0),
        "grad_out": centred(seeds[10], (SEQ, H * VDIM), 1.0, 6.0, ((0, 16), (1, 2))),
    }


EPSILON = 1e-06
ROTARY_BASE = 10000.0

def rounded(values):
    return lax.optimization_barrier(values.astype(jnp.bfloat16)).astype(jnp.float32)

def rotation(positions):
    pair_count = ROPE // 2
    frequency = ROTARY_BASE ** (-jnp.arange(pair_count, dtype=jnp.float32) / pair_count)
    angles = positions.astype(jnp.float32)[:, None] * frequency[None, :]
    return (jnp.cos(angles), jnp.sin(angles))

def rotate_pairs(values, cos_table, sin_table):
    pair_count = ROPE // 2
    first_half = values[..., :pair_count]
    second_half = values[..., pair_count:]
    return jnp.concatenate([first_half * cos_table - second_half * sin_table, first_half * sin_table + second_half * cos_table], axis=-1)

def unrotate(values, cos_table, sin_table):
    pair_count = ROPE // 2
    first_half = values[..., :pair_count]
    second_half = values[..., pair_count:]
    return jnp.concatenate([first_half * cos_table + second_half * sin_table, second_half * cos_table - first_half * sin_table], axis=-1)

def to_positions(values):
    half_rows = values.shape[0] // (2 * N_CTX)
    trailing = values.shape[1:]
    shaped = values.reshape((N_CTX, 2, half_rows) + trailing)
    early_rows = shaped[:, 0].reshape((N_CTX * half_rows,) + trailing)
    late_rows = shaped[::-1, 1].reshape((N_CTX * half_rows,) + trailing)
    return jnp.concatenate([early_rows, late_rows], axis=0)

def to_rows(values):
    half_rows = values.shape[0] // (2 * N_CTX)
    trailing = values.shape[1:]
    early_rows = values[:N_CTX * half_rows].reshape((N_CTX, half_rows) + trailing)
    late_rows = values[N_CTX * half_rows:].reshape((N_CTX, half_rows) + trailing)[::-1]
    return jnp.stack([early_rows, late_rows], axis=1).reshape((2 * N_CTX * half_rows,) + trailing)

def reference(hidden, embed, gain_hidden, gain_embed, proj_hidden, proj_embed, gain_latent, key_up, value_up, queries, grad_out):
    seq_total = hidden.shape[0]
    head_count = key_up.shape[1] // NOPE
    score_scale = (NOPE + ROPE) ** (-0.5)
    key_block = max(256, seq_total // 16)
    hidden_pos = to_positions(hidden)
    embed_pos = to_positions(embed)
    next_embed = jnp.concatenate([embed_pos[1:], jnp.zeros((1, embed.shape[1]), embed.dtype)], axis=0)
    hidden_wide = hidden_pos.astype(jnp.float32)
    next_wide = next_embed.astype(jnp.float32)
    inv_hidden = lax.rsqrt(lax.optimization_barrier(jnp.sum(hidden_wide * hidden_wide, axis=1, keepdims=True)) / D + EPSILON)
    inv_next = lax.rsqrt(lax.optimization_barrier(jnp.sum(next_wide * next_wide, axis=1, keepdims=True)) / D + EPSILON)
    scaled_hidden = (hidden_wide * gain_hidden).astype(jnp.bfloat16)
    scaled_next = (next_wide * gain_embed).astype(jnp.bfloat16)
    part_hidden = jnp.dot(scaled_hidden, proj_hidden, preferred_element_type=jnp.float32)
    part_next = jnp.dot(scaled_next, proj_embed, preferred_element_type=jnp.float32)
    latent = inv_hidden * part_hidden + inv_next * part_next
    leading = latent[:, :LAT]
    inv_latent = lax.rsqrt(lax.optimization_barrier(jnp.mean(leading * leading, axis=1, keepdims=True)) + EPSILON)
    key_latent = (leading * inv_latent * gain_latent).astype(jnp.bfloat16)
    positions = jnp.arange(seq_total, dtype=jnp.int32)
    cos_table, sin_table = rotation(positions)
    key_rope = rotate_pairs(latent[:, LAT:], cos_table, sin_table).astype(jnp.bfloat16)
    key_table = jnp.concatenate([key_latent, key_rope], axis=1)
    query_heads = to_positions(queries).reshape(seq_total, head_count, NOPE + ROPE).astype(jnp.float32)
    query_rot = rotate_pairs(query_heads[..., NOPE:], cos_table[:, None], sin_table[:, None]).astype(jnp.bfloat16)
    key_up_heads = key_up.reshape(LAT, head_count, NOPE).astype(jnp.float32)
    value_up_heads = value_up.reshape(LAT, head_count, VDIM).astype(jnp.float32)
    query_latent = jnp.einsum('shn,lhn->shl', query_heads[..., :NOPE], key_up_heads).astype(jnp.bfloat16)
    query_full = jnp.swapaxes(jnp.concatenate([query_latent, query_rot], axis=2), 0, 1)
    grad_heads = to_positions(grad_out).reshape(seq_total, head_count, VDIM).astype(jnp.float32)
    grad_latent = jnp.swapaxes(jnp.einsum('shv,lhv->shl', grad_heads, value_up_heads).astype(jnp.bfloat16), 0, 1)
    grad_keys = jnp.zeros((seq_total, LAT + ROPE), jnp.float32)
    out_blocks = []
    grad_query_blocks = []
    for block_index in range(seq_total // key_block):
        first_row = block_index * key_block
        last_row = first_row + key_block
        key_slab = key_table[:last_row].astype(jnp.float32)
        allowed = jnp.arange(last_row, dtype=jnp.int32)[None, :] <= jnp.arange(first_row, last_row, dtype=jnp.int32)[:, None]

        def per_head(state_keys, inputs):
            query_block, grad_block = inputs
            query_wide = query_block.astype(jnp.float32)
            grad_wide = grad_block.astype(jnp.float32)
            scores = jnp.dot(query_wide, key_slab.T, preferred_element_type=jnp.float32) * score_scale
            scores = jnp.where(allowed, scores, -jnp.inf)
            weights = jnp.exp(scores - lax.optimization_barrier(jnp.max(scores, axis=1, keepdims=True)))
            prob_wide = rounded(weights / lax.optimization_barrier(jnp.sum(weights, axis=1, keepdims=True)))
            out_latent = jnp.dot(prob_wide, key_slab[:, :LAT], preferred_element_type=jnp.float32)
            delta_rows = lax.optimization_barrier(jnp.sum(grad_wide * out_latent, axis=1, keepdims=True))
            grad_prob = jnp.dot(grad_wide, key_slab[:, :LAT].T, preferred_element_type=jnp.float32)
            grad_score = rounded(prob_wide * (grad_prob - delta_rows) * score_scale)
            grad_query = jnp.dot(grad_score, key_slab, preferred_element_type=jnp.float32)
            grad_lead = jnp.dot(grad_score.T, query_wide[:, :LAT], preferred_element_type=jnp.float32) + jnp.dot(prob_wide.T, grad_wide, preferred_element_type=jnp.float32)
            grad_tail = jnp.dot(grad_score.T, query_wide[:, LAT:], preferred_element_type=jnp.float32)
            return (state_keys + jnp.concatenate([grad_lead, grad_tail], axis=1), (out_latent.astype(jnp.bfloat16), grad_query))
        block_keys, (out_heads, grad_heads_q) = lax.scan(per_head, jnp.zeros((last_row, LAT + ROPE), jnp.float32), (query_full[:, first_row:last_row], grad_latent[:, first_row:last_row]))
        grad_keys = grad_keys + jnp.pad(block_keys, ((0, seq_total - last_row), (0, 0)))
        out_blocks.append(out_heads)
        grad_query_blocks.append(grad_heads_q)
    out_all = jnp.concatenate(out_blocks, axis=1)
    grad_query_all = jnp.concatenate(grad_query_blocks, axis=1)
    attended = jnp.einsum('hsl,lhv->shv', out_all.astype(jnp.float32), value_up_heads).astype(jnp.bfloat16).reshape(seq_total, head_count * VDIM)
    grad_lead_q = rounded(grad_query_all[..., :LAT])
    grad_nope = jnp.einsum('hsl,lhn->shn', grad_lead_q, key_up_heads)
    grad_rope = unrotate(jnp.swapaxes(grad_query_all[..., LAT:], 0, 1), cos_table[:, None], sin_table[:, None])
    grad_queries = jnp.concatenate([grad_nope, grad_rope], axis=2).astype(jnp.bfloat16).reshape(seq_total, head_count * (NOPE + ROPE))
    grad_rope_key = unrotate(grad_keys[:, LAT:], cos_table, sin_table)
    gained = gain_latent * grad_keys[:, :LAT]
    grad_leading = inv_latent * gained - inv_latent ** 3 * leading * lax.optimization_barrier(jnp.sum(gained * leading, axis=1, keepdims=True)) / LAT
    grad_lat = jnp.concatenate([grad_leading, grad_rope_key], axis=1)
    part_grad_hidden = (inv_hidden * grad_lat).astype(jnp.bfloat16)
    part_grad_next = (inv_next * grad_lat).astype(jnp.bfloat16)
    coef_hidden = lax.optimization_barrier(jnp.sum(grad_lat * part_hidden, axis=1, keepdims=True)) * inv_hidden ** 3 / D
    coef_next = lax.optimization_barrier(jnp.sum(grad_lat * part_next, axis=1, keepdims=True)) * inv_next ** 3 / D
    grad_hidden = (gain_hidden * jnp.dot(part_grad_hidden, proj_hidden.T, preferred_element_type=jnp.float32) - coef_hidden * hidden_wide).astype(jnp.bfloat16)
    grad_next = gain_embed * jnp.dot(part_grad_next, proj_embed.T, preferred_element_type=jnp.float32) - coef_next * next_wide
    grad_embed = jnp.concatenate([jnp.zeros((1, grad_next.shape[1]), jnp.float32), grad_next[:-1]], axis=0).astype(jnp.bfloat16)
    return (to_rows(attended), to_rows(grad_queries), to_rows(grad_hidden), to_rows(grad_embed))
```

```python
import functools

import jax
import jax.numpy as jnp
from jax import lax
from jax.experimental import pallas as pl
from jax.experimental.pallas import tpu as pltpu
from jax.sharding import PartitionSpec as P

D = 7168
LAT = 512
ROPE = 64
NOPE = 128
VDIM = 128


EPSILON = 1e-06
ROTARY_BASE = 10000.0


def with_halo(x, sides, width):
    for axis, dim in sides:
        size, length = (lax.axis_size(axis), x.shape[dim])
        up = [(i, (i + 1) % size) for i in range(size - 1)]
        down = [(j, i) for i, j in up]
        last = lax.slice_in_dim(x, length - width, length, axis=dim)
        first = lax.slice_in_dim(x, 0, width, axis=dim)
        before = lax.ppermute(last, axis, up)
        after = lax.ppermute(first, axis, down)
        x = jnp.concatenate([before, x, after], axis=dim)
    return x


def rotation(positions):
    pair_count = ROPE // 2
    frequency = ROTARY_BASE ** (-jnp.arange(pair_count, dtype=jnp.float32) / pair_count)
    angles = positions.astype(jnp.float32)[:, None] * frequency[None, :]
    return (jnp.cos(angles), jnp.sin(angles))


def rotate_pairs(values, cos_table, sin_table):
    pair_count = ROPE // 2
    first_half = values[..., :pair_count]
    second_half = values[..., pair_count:]
    return jnp.concatenate(
        [
            first_half * cos_table - second_half * sin_table,
            first_half * sin_table + second_half * cos_table,
        ],
        axis=-1,
    )


def unrotate(values, cos_table, sin_table):
    pair_count = ROPE // 2
    first_half = values[..., :pair_count]
    second_half = values[..., pair_count:]
    return jnp.concatenate(
        [
            first_half * cos_table + second_half * sin_table,
            second_half * cos_table - first_half * sin_table,
        ],
        axis=-1,
    )


def local_positions(tokens, ctx_index, groups):
    half_rows = tokens // 2
    offsets = jnp.arange(tokens, dtype=jnp.int32)
    early_pos = ctx_index * half_rows + offsets
    late_pos = (2 * groups - 1 - ctx_index) * half_rows + offsets - half_rows
    return jnp.where(offsets < half_rows, early_pos, late_pos)


def finish_latent(part_hidden, part_next, squares, gain_latent, positions):
    inverse = lax.rsqrt(squares / D + EPSILON)
    latent = inverse[:, 0:1] * part_hidden + inverse[:, 1:2] * part_next
    leading = latent[:, :LAT]
    inv_latent = lax.rsqrt(jnp.mean(leading * leading, axis=1, keepdims=True) + EPSILON)
    key_latent = (leading * inv_latent * gain_latent).astype(jnp.bfloat16)
    cos_table, sin_table = rotation(positions)
    key_rope = rotate_pairs(latent[:, LAT:], cos_table, sin_table).astype(jnp.bfloat16)
    return (key_latent, key_rope, latent, inverse, inv_latent)


def latent_backward(
    grad_key_latent,
    grad_key_rope,
    latent,
    inverse,
    inv_latent,
    gain_latent,
    positions,
    part_hidden,
    part_next,
):
    cos_table, sin_table = rotation(positions)
    grad_rope = unrotate(grad_key_rope, cos_table, sin_table)
    leading = latent[:, :LAT]
    gained = gain_latent * grad_key_latent
    grad_leading = (
        inv_latent * gained
        - inv_latent**3 * leading * jnp.sum(gained * leading, axis=1, keepdims=True) / LAT
    )
    grad_latent = jnp.concatenate([grad_leading, grad_rope], axis=1)
    part_grad_hidden = (inverse[:, 0:1] * grad_latent).astype(jnp.bfloat16)
    part_grad_next = (inverse[:, 1:2] * grad_latent).astype(jnp.bfloat16)
    inv_sums = jnp.concatenate(
        [
            jnp.sum(grad_latent * part_hidden, axis=1, keepdims=True),
            jnp.sum(grad_latent * part_next, axis=1, keepdims=True),
        ],
        axis=1,
    )
    coefficient = inv_sums * inverse**3 / D
    return (part_grad_hidden, part_grad_next, coefficient)


def group_size(head_count):
    for size in (4, 2, 1):
        if head_count % size == 0:
            return size


def attention_kernel(
    groups,
    group,
    key_block,
    score_scale,
    keys_ref,
    queries_ref,
    grad_out_ref,
    key_up_ref,
    value_up_ref,
    cos_ref,
    sin_ref,
    attended_ref,
    grad_queries_ref,
    grad_keys_ref,
    table,
    table_t,
    query_rows,
    grad_rows,
    score_buf,
    dprob_buf,
    out_acc,
    dquery_acc,
    dkey_acc,
):
    step = pl.program_id(0)
    ctx_index = lax.axis_index("ctx")
    tokens = queries_ref.shape[0]
    half_rows = tokens // 2
    rows = group * half_rows
    key_total = keys_ref.shape[0]
    width = LAT + ROPE
    padded = table.shape[1]
    blocks = key_total // key_block
    chunk_rows = [
        (2 * c if c < groups else 2 * (2 * groups - 1 - c) + 1) * half_rows
        for c in range(2 * groups)
    ]

    @pl.when(step == 0)
    def _():
        dkey_acc[...] = jnp.zeros_like(dkey_acc)
        query_rows[...] = jnp.zeros_like(query_rows)
        for c, row in enumerate(chunk_rows):
            chunk = keys_ref[row : row + half_rows, :]
            pad = jnp.zeros((half_rows, padded - width), chunk.dtype)
            table[c * half_rows : (c + 1) * half_rows, :] = jnp.concatenate([chunk, pad], axis=1)

        @pl.loop(0, blocks)
        def _(j):
            first = pl.multiple_of(j * key_block, key_block)
            table_t[j] = table[pl.ds(first, key_block), :].T

    cos2 = cos_ref[...]
    sin2 = sin_ref[...]
    half = ROPE // 2
    nt = (((1,), (1,)), ((), ()))
    tn = (((0,), (0,)), ((), ()))
    all_queries = queries_ref[...]
    for g in range(group):
        first = g * (NOPE + ROPE)
        nope = all_queries[:, first : first + NOPE]
        rope = all_queries[:, first + NOPE : first + NOPE + ROPE].astype(jnp.float32)
        swapped = jnp.concatenate([-rope[:, half:], rope[:, :half]], axis=1)
        rotated = (rope * cos2 + swapped * sin2).astype(jnp.bfloat16)
        lead = lax.dot_general(
            nope, key_up_ref[:, g * NOPE : (g + 1) * NOPE], nt, preferred_element_type=jnp.float32
        ).astype(jnp.bfloat16)
        grads = lax.dot_general(
            grad_out_ref[:, g * VDIM : (g + 1) * VDIM],
            value_up_ref[:, g * VDIM : (g + 1) * VDIM],
            nt,
            preferred_element_type=jnp.float32,
        ).astype(jnp.bfloat16)
        for h in range(2):
            source = slice(h * half_rows, (h + 1) * half_rows)
            target = slice(g * half_rows, (g + 1) * half_rows)
            query_rows[h, target, :LAT] = lead[source]
            query_rows[h, target, LAT : LAT + ROPE] = rotated[source]
            grad_rows[h, target, :] = grads[source]

    for h in range(2):
        first_pos = (ctx_index if h == 0 else 2 * groups - 1 - ctx_index) * half_rows
        block_count = (first_pos + half_rows + key_block - 1) // key_block
        row_pos = first_pos + lax.broadcasted_iota(jnp.int32, (rows, key_block), 0) % half_rows
        key_off = lax.broadcasted_iota(jnp.int32, (rows, key_block), 1)
        gap = row_pos - key_off
        lanes = 128

        def fold(values, op):
            total = values[:, :lanes]
            for k in range(1, key_block // lanes):
                total = op(total, values[:, k * lanes : (k + 1) * lanes])
            return total

        def score_step(j, running):
            scores = jnp.dot(query_rows[h], table_t[j], preferred_element_type=jnp.float32)
            scores = jnp.where(gap >= j * key_block, scores, -1e30)
            score_buf[j] = scores
            dprob_buf[j] = jnp.dot(
                grad_rows[h], table_t[j, :LAT, :], preferred_element_type=jnp.float32
            )
            return jnp.maximum(running, fold(scores, jnp.maximum))

        running = lax.fori_loop(
            0, block_count, score_step, jnp.full((rows, lanes), -1e30, jnp.float32)
        )
        row_max = jnp.max(running, axis=1, keepdims=True)

        def weight_step(j, sums):
            weights = jnp.exp((score_buf[j] - row_max) * score_scale)
            score_buf[j] = weights
            return (
                sums[0] + fold(weights, jnp.add),
                sums[1] + fold(weights * dprob_buf[j], jnp.add),
            )

        zeros = jnp.zeros((rows, lanes), jnp.float32)
        weight_sum, delta_sum = lax.fori_loop(0, block_count, weight_step, (zeros, zeros))
        inv_sum = 1.0 / jnp.sum(weight_sum, axis=1, keepdims=True)
        delta = jnp.sum(delta_sum, axis=1, keepdims=True) * inv_sum
        out_acc[...] = jnp.zeros_like(out_acc)
        dquery_acc[...] = jnp.zeros_like(dquery_acc)

        def grad_step(j, carry):
            first = pl.multiple_of(j * key_block, key_block)
            prob = (score_buf[j] * inv_sum).astype(jnp.bfloat16)
            dscore = (
                prob.astype(jnp.float32) * (dprob_buf[j] - delta) * score_scale
            ).astype(jnp.bfloat16)
            keys = table[pl.ds(first, key_block), :]
            out_acc[...] += jnp.dot(prob, keys[:, :LAT], preferred_element_type=jnp.float32)
            dquery_acc[...] += jnp.dot(dscore, keys, preferred_element_type=jnp.float32)
            dkey_acc[pl.ds(first, key_block), :] += lax.dot_general(
                dscore, query_rows[h], tn, preferred_element_type=jnp.float32
            )
            dkey_acc[pl.ds(first, key_block), :LAT] += lax.dot_general(
                prob, grad_rows[h], tn, preferred_element_type=jnp.float32
            )
            return carry

        lax.fori_loop(0, block_count, grad_step, 0)
        token = slice(h * half_rows, (h + 1) * half_rows)
        pieces = []
        for g in range(group):
            part = slice(g * half_rows, (g + 1) * half_rows)
            attended_ref[token, g * VDIM : (g + 1) * VDIM] = jnp.dot(
                out_acc[part, :].astype(jnp.bfloat16),
                value_up_ref[:, g * VDIM : (g + 1) * VDIM],
                preferred_element_type=jnp.float32,
            ).astype(jnp.bfloat16)
            pieces.append(
                jnp.dot(
                    dquery_acc[part, :LAT].astype(jnp.bfloat16),
                    key_up_ref[:, g * NOPE : (g + 1) * NOPE],
                    preferred_element_type=jnp.float32,
                )
            )
            tail = dquery_acc[part, LAT : LAT + ROPE]
            swapped = jnp.concatenate([tail[:, half:], -tail[:, :half]], axis=1)
            pieces.append(tail * cos2[token] + swapped * sin2[token])
        grad_queries_ref[token, :] = jnp.concatenate(pieces, axis=1).astype(jnp.bfloat16)

    @pl.when(step == pl.num_programs(0) - 1)
    def _():
        for c, row in enumerate(chunk_rows):
            grad_keys_ref[row : row + half_rows, :] = dkey_acc[
                c * half_rows : (c + 1) * half_rows, :width
            ].astype(grad_keys_ref.dtype)


def attention(keys, queries, grad_out, key_up, value_up, cos2, sin2, groups):
    tokens = queries.shape[0]
    half_rows = tokens // 2
    head_count = key_up.shape[1] // NOPE
    group = group_size(head_count)
    key_total = keys.shape[0]
    key_block = 256
    blocks = key_total // key_block
    padded = LAT + 2 * ROPE
    rows = group * half_rows
    body = functools.partial(
        attention_kernel, groups, group, key_block, (NOPE + ROPE) ** (-0.5)
    )
    whole = lambda shape: pl.BlockSpec(shape, lambda i: (0, 0), pipeline_mode=pl.Buffered(1))
    column = lambda height, width: pl.BlockSpec((height, group * width), lambda i: (0, i))
    return pl.pallas_call(
        body,
        grid=(head_count // group,),
        in_specs=[
            whole(keys.shape),
            column(tokens, NOPE + ROPE),
            column(tokens, VDIM),
            column(LAT, NOPE),
            column(LAT, VDIM),
            whole(cos2.shape),
            whole(sin2.shape),
        ],
        out_specs=[
            column(tokens, VDIM),
            column(tokens, NOPE + ROPE),
            whole(keys.shape),
        ],
        out_shape=[
            jax.ShapeDtypeStruct((tokens, head_count * VDIM), jnp.bfloat16),
            jax.ShapeDtypeStruct((tokens, head_count * (NOPE + ROPE)), jnp.bfloat16),
            jax.ShapeDtypeStruct(keys.shape, jnp.bfloat16),
        ],
        scratch_shapes=[
            pltpu.VMEM((key_total, padded), jnp.bfloat16),
            pltpu.VMEM((blocks, padded, key_block), jnp.bfloat16),
            pltpu.VMEM((2, rows, padded), jnp.bfloat16),
            pltpu.VMEM((2, rows, LAT), jnp.bfloat16),
            pltpu.VMEM((blocks, rows, key_block), jnp.float32),
            pltpu.VMEM((blocks, rows, key_block), jnp.float32),
            pltpu.VMEM((rows, LAT), jnp.float32),
            pltpu.VMEM((rows, padded), jnp.float32),
            pltpu.VMEM((key_total, padded), jnp.float32),
        ],
        compiler_params=pltpu.CompilerParams(
            dimension_semantics=("arbitrary",), vmem_limit_bytes=60 * 1024 * 1024
        ),
        name="attention",
    )(keys, queries, grad_out, key_up, value_up, cos2, sin2)


def pair_sum(values):
    if lax.axis_size("tp") != 2:
        return lax.psum(values, "tp")
    return tuple(v + lax.ppermute(v, "tp", [(0, 1), (1, 0)]) for v in values)


def on_device(
    hidden,
    embed,
    gain_hidden,
    gain_embed,
    proj_hidden,
    proj_embed,
    gain_latent,
    key_up,
    value_up,
    queries,
    grad_out,
):
    tokens = hidden.shape[0]
    half_rows = tokens // 2
    groups = lax.axis_size("ctx")
    ctx_index = lax.axis_index("ctx")
    edge_rows = jnp.stack([embed[0], embed[half_rows]], axis=0)
    padded = with_halo(edge_rows, (("ctx", 0),), 1)
    after_early = jnp.where(ctx_index == groups - 1, embed[half_rows], padded[3])
    next_embed = jnp.concatenate(
        [embed[1:half_rows], after_early[None], embed[half_rows + 1 :], padded[0][None]], axis=0
    )
    hidden_wide = hidden.astype(jnp.float32)
    next_wide = next_embed.astype(jnp.float32)
    squares = jnp.stack(
        [jnp.sum(hidden_wide * hidden_wide, axis=1), jnp.sum(next_wide * next_wide, axis=1)], axis=1
    )
    scaled_hidden = (hidden_wide * gain_hidden).astype(jnp.bfloat16)
    scaled_next = (next_wide * gain_embed).astype(jnp.bfloat16)
    part_hidden = jnp.dot(scaled_hidden, proj_hidden, preferred_element_type=jnp.float32)
    part_next = jnp.dot(scaled_next, proj_embed, preferred_element_type=jnp.float32)
    positions = local_positions(tokens, ctx_index, groups)
    part_hidden, part_next, squares = pair_sum((part_hidden, part_next, squares))
    key_latent, key_rope, latent, inverse, inv_latent = finish_latent(
        part_hidden, part_next, squares, gain_latent, positions
    )
    keys = lax.all_gather(
        jnp.concatenate([key_latent, key_rope], axis=1), "ctx", axis=0, tiled=True
    )
    cos_table, sin_table = rotation(positions)
    attended, grad_queries, grad_keys = attention(
        keys,
        queries,
        grad_out,
        key_up,
        value_up,
        jnp.concatenate([cos_table, cos_table], axis=1),
        jnp.concatenate([sin_table, sin_table], axis=1),
        groups,
    )
    grad_keys = lax.psum_scatter(grad_keys, "ctx", scatter_dimension=0, tiled=True)
    if lax.axis_size("tp") == 2:
        other = lax.ppermute(grad_keys, "tp", [(0, 1), (1, 0)])
        grad_keys = grad_keys.astype(jnp.float32) + other.astype(jnp.float32)
    else:
        grad_keys = lax.psum(grad_keys.astype(jnp.float32), "tp")
    grad_key_latent, grad_key_rope = grad_keys[:, :LAT], grad_keys[:, LAT:]
    part_grad_hidden, part_grad_next, coefficient = latent_backward(
        grad_key_latent,
        grad_key_rope,
        latent,
        inverse,
        inv_latent,
        gain_latent,
        positions,
        part_hidden,
        part_next,
    )
    grad_hidden = (
        gain_hidden
        * jnp.einsum("rc,dc->rd", part_grad_hidden, proj_hidden, preferred_element_type=jnp.float32)
        - coefficient[:, 0:1] * hidden_wide
    ).astype(jnp.bfloat16)
    grad_next = (
        gain_embed
        * jnp.einsum("rc,dc->rd", part_grad_next, proj_embed, preferred_element_type=jnp.float32)
        - coefficient[:, 1:2] * next_wide
    )
    grad_next_rounded = grad_next.astype(jnp.bfloat16)
    edge_grads = jnp.stack(
        [grad_next_rounded[tokens - 1], grad_next_rounded[half_rows - 1]], axis=0
    )
    returned = with_halo(edge_grads, (("ctx", 0),), 1)
    before_late = jnp.where(ctx_index == groups - 1, grad_next_rounded[half_rows - 1], returned[3])
    grad_embed = jnp.concatenate(
        [
            returned[0][None],
            grad_next_rounded[: half_rows - 1],
            before_late[None],
            grad_next_rounded[half_rows : tokens - 1],
        ],
        axis=0,
    )
    return (attended, grad_queries, grad_hidden, grad_embed)


def solution(mesh):
    placed = (
        P("ctx", "tp"),
        P("ctx", "tp"),
        P("tp"),
        P("tp"),
        P("tp", None),
        P("tp", None),
        P(),
        P(None, "tp"),
        P(None, "tp"),
        P("ctx", "tp"),
        P("ctx", "tp"),
    )
    return jax.shard_map(
        on_device,
        mesh=mesh,
        in_specs=placed,
        out_specs=(P("ctx", "tp"), P("ctx", "tp"), P("ctx", "tp"), P("ctx", "tp")),
        check_vma=False,
    )
```

```python
import functools

import jax
import jax.numpy as jnp
from jax import lax
from jax.experimental import pallas as pl
from jax.experimental.pallas import tpu as pltpu
from jax.sharding import PartitionSpec as P

D = 7168
LAT = 512
ROPE = 64
NOPE = 128
VDIM = 128


EPSILON = 1e-06
ROTARY_BASE = 10000.0


def with_halo(x, sides, width):
    for axis, dim in sides:
        size, length = (lax.axis_size(axis), x.shape[dim])
        up = [(i, (i + 1) % size) for i in range(size - 1)]
        down = [(j, i) for i, j in up]
        last = lax.slice_in_dim(x, length - width, length, axis=dim)
        first = lax.slice_in_dim(x, 0, width, axis=dim)
        before = lax.ppermute(last, axis, up)
        after = lax.ppermute(first, axis, down)
        x = jnp.concatenate([before, x, after], axis=dim)
    return x


def rotation(positions):
    pair_count = ROPE // 2
    frequency = ROTARY_BASE ** (-jnp.arange(pair_count, dtype=jnp.float32) / pair_count)
    angles = positions.astype(jnp.float32)[:, None] * frequency[None, :]
    return (jnp.cos(angles), jnp.sin(angles))


def rotate_pairs(values, cos_table, sin_table):
    pair_count = ROPE // 2
    first_half = values[..., :pair_count]
    second_half = values[..., pair_count:]
    return jnp.concatenate(
        [
            first_half * cos_table - second_half * sin_table,
            first_half * sin_table + second_half * cos_table,
        ],
        axis=-1,
    )


def unrotate(values, cos_table, sin_table):
    pair_count = ROPE // 2
    first_half = values[..., :pair_count]
    second_half = values[..., pair_count:]
    return jnp.concatenate(
        [
            first_half * cos_table + second_half * sin_table,
            second_half * cos_table - first_half * sin_table,
        ],
        axis=-1,
    )


def local_positions(tokens, ctx_index, groups):
    half_rows = tokens // 2
    offsets = jnp.arange(tokens, dtype=jnp.int32)
    early_pos = ctx_index * half_rows + offsets
    late_pos = (2 * groups - 1 - ctx_index) * half_rows + offsets - half_rows
    return jnp.where(offsets < half_rows, early_pos, late_pos)


def finish_latent(part_hidden, part_next, squares, gain_latent, positions):
    inverse = lax.rsqrt(squares / D + EPSILON)
    latent = inverse[:, 0:1] * part_hidden + inverse[:, 1:2] * part_next
    leading = latent[:, :LAT]
    inv_latent = lax.rsqrt(jnp.mean(leading * leading, axis=1, keepdims=True) + EPSILON)
    key_latent = (leading * inv_latent * gain_latent).astype(jnp.bfloat16)
    cos_table, sin_table = rotation(positions)
    key_rope = rotate_pairs(latent[:, LAT:], cos_table, sin_table).astype(jnp.bfloat16)
    return (key_latent, key_rope, latent, inverse, inv_latent)


def latent_backward(
    grad_key_latent,
    grad_key_rope,
    latent,
    inverse,
    inv_latent,
    gain_latent,
    positions,
    part_hidden,
    part_next,
):
    cos_table, sin_table = rotation(positions)
    grad_rope = unrotate(grad_key_rope, cos_table, sin_table)
    leading = latent[:, :LAT]
    gained = gain_latent * grad_key_latent
    grad_leading = (
        inv_latent * gained
        - inv_latent**3 * leading * jnp.sum(gained * leading, axis=1, keepdims=True) / LAT
    )
    grad_latent = jnp.concatenate([grad_leading, grad_rope], axis=1)
    part_grad_hidden = (inverse[:, 0:1] * grad_latent).astype(jnp.bfloat16)
    part_grad_next = (inverse[:, 1:2] * grad_latent).astype(jnp.bfloat16)
    inv_sums = jnp.concatenate(
        [
            jnp.sum(grad_latent * part_hidden, axis=1, keepdims=True),
            jnp.sum(grad_latent * part_next, axis=1, keepdims=True),
        ],
        axis=1,
    )
    coefficient = inv_sums * inverse**3 / D
    return (part_grad_hidden, part_grad_next, coefficient)


def group_size(head_count):
    for size in (4, 2, 1):
        if head_count % size == 0:
            return size


def attention_kernel(
    groups,
    group,
    key_block,
    score_scale,
    keys_ref,
    queries_ref,
    grad_out_ref,
    key_up_ref,
    value_up_ref,
    cos_ref,
    sin_ref,
    attended_ref,
    grad_queries_ref,
    grad_keys_ref,
    table,
    table_t,
    query_rows,
    grad_rows,
    score_buf,
    dprob_buf,
    out_acc,
    dquery_acc,
    dkey_acc,
):
    step = pl.program_id(0)
    ctx_index = lax.axis_index("ctx")
    tokens = queries_ref.shape[0]
    half_rows = tokens // 2
    rows = group * half_rows
    key_total = table.shape[0]
    width = LAT + ROPE
    padded = table.shape[1]
    blocks = key_total // key_block
    quarter = half_rows // 2
    pieces_of = [
        (2 * c + part, (part, d % 2, y, (d // 2) % 2, d // 4))
        for c in range(2 * groups)
        for y, d in [(0, c) if c < groups else (1, 2 * groups - 1 - c)]
        for part in range(2)
    ]

    @pl.when(step == 0)
    def _():
        dkey_acc[...] = jnp.zeros_like(dkey_acc)
        query_rows[...] = jnp.zeros_like(query_rows)
        for piece, slot in pieces_of:
            chunk = keys_ref[slot]
            pad = jnp.zeros((quarter, padded - width), chunk.dtype)
            table[piece * quarter : (piece + 1) * quarter, :] = jnp.concatenate(
                [chunk, pad], axis=1
            )

        @pl.loop(0, blocks)
        def _(j):
            first = pl.multiple_of(j * key_block, key_block)
            table_t[j] = table[pl.ds(first, key_block), :].T

    cos2 = cos_ref[...]
    sin2 = sin_ref[...]
    half = ROPE // 2
    nt = (((1,), (1,)), ((), ()))
    tn = (((0,), (0,)), ((), ()))
    all_queries = queries_ref[...]
    for g in range(group):
        first = g * (NOPE + ROPE)
        nope = all_queries[:, first : first + NOPE]
        rope = all_queries[:, first + NOPE : first + NOPE + ROPE].astype(jnp.float32)
        swapped = jnp.concatenate([-rope[:, half:], rope[:, :half]], axis=1)
        rotated = (rope * cos2 + swapped * sin2).astype(jnp.bfloat16)
        lead = lax.dot_general(
            nope, key_up_ref[:, g * NOPE : (g + 1) * NOPE], nt, preferred_element_type=jnp.float32
        ).astype(jnp.bfloat16)
        grads = lax.dot_general(
            grad_out_ref[:, g * VDIM : (g + 1) * VDIM],
            value_up_ref[:, g * VDIM : (g + 1) * VDIM],
            nt,
            preferred_element_type=jnp.float32,
        ).astype(jnp.bfloat16)
        for h in range(2):
            source = slice(h * half_rows, (h + 1) * half_rows)
            target = slice(g * half_rows, (g + 1) * half_rows)
            query_rows[h, target, :LAT] = lead[source]
            query_rows[h, target, LAT : LAT + ROPE] = rotated[source]
            grad_rows[h, target, :] = grads[source]

    for h in range(2):
        first_pos = (ctx_index if h == 0 else 2 * groups - 1 - ctx_index) * half_rows
        block_count = (first_pos + half_rows + key_block - 1) // key_block
        row_pos = first_pos + lax.broadcasted_iota(jnp.int32, (rows, key_block), 0) % half_rows
        key_off = lax.broadcasted_iota(jnp.int32, (rows, key_block), 1)
        gap = row_pos - key_off
        lanes = 128

        def fold(values, op):
            total = values[:, :lanes]
            for k in range(1, key_block // lanes):
                total = op(total, values[:, k * lanes : (k + 1) * lanes])
            return total

        def score_step(j, running):
            scores = jnp.dot(query_rows[h], table_t[j], preferred_element_type=jnp.float32)
            scores = jnp.where(gap >= j * key_block, scores, -1e30)
            score_buf[j] = scores
            dprob_buf[j] = jnp.dot(
                grad_rows[h], table_t[j, :LAT, :], preferred_element_type=jnp.float32
            )
            return jnp.maximum(running, fold(scores, jnp.maximum))

        running = lax.fori_loop(
            0, block_count, score_step, jnp.full((rows, lanes), -1e30, jnp.float32)
        )
        row_max = jnp.max(running, axis=1, keepdims=True)

        def weight_step(j, sums):
            weights = jnp.exp((score_buf[j] - row_max) * score_scale)
            score_buf[j] = weights
            return (
                sums[0] + fold(weights, jnp.add),
                sums[1] + fold(weights * dprob_buf[j], jnp.add),
            )

        zeros = jnp.zeros((rows, lanes), jnp.float32)
        weight_sum, delta_sum = lax.fori_loop(0, block_count, weight_step, (zeros, zeros))
        inv_sum = 1.0 / jnp.sum(weight_sum, axis=1, keepdims=True)
        delta = jnp.sum(delta_sum, axis=1, keepdims=True) * inv_sum
        out_acc[...] = jnp.zeros_like(out_acc)
        dquery_acc[...] = jnp.zeros_like(dquery_acc)

        def grad_step(j, carry):
            first = pl.multiple_of(j * key_block, key_block)
            prob = (score_buf[j] * inv_sum).astype(jnp.bfloat16)
            dscore = (
                prob.astype(jnp.float32) * (dprob_buf[j] - delta) * score_scale
            ).astype(jnp.bfloat16)
            keys = table[pl.ds(first, key_block), :]
            out_acc[...] += jnp.dot(prob, keys[:, :LAT], preferred_element_type=jnp.float32)
            dquery_acc[...] += jnp.dot(dscore, keys, preferred_element_type=jnp.float32)
            dkey_acc[pl.ds(first, key_block), :] += lax.dot_general(
                dscore, query_rows[h], tn, preferred_element_type=jnp.float32
            )
            dkey_acc[pl.ds(first, key_block), :LAT] += lax.dot_general(
                prob, grad_rows[h], tn, preferred_element_type=jnp.float32
            )
            return carry

        lax.fori_loop(0, block_count, grad_step, 0)
        token = slice(h * half_rows, (h + 1) * half_rows)
        pieces = []
        for g in range(group):
            part = slice(g * half_rows, (g + 1) * half_rows)
            attended_ref[token, g * VDIM : (g + 1) * VDIM] = jnp.dot(
                out_acc[part, :].astype(jnp.bfloat16),
                value_up_ref[:, g * VDIM : (g + 1) * VDIM],
                preferred_element_type=jnp.float32,
            ).astype(jnp.bfloat16)
            pieces.append(
                jnp.dot(
                    dquery_acc[part, :LAT].astype(jnp.bfloat16),
                    key_up_ref[:, g * NOPE : (g + 1) * NOPE],
                    preferred_element_type=jnp.float32,
                )
            )
            tail = dquery_acc[part, LAT : LAT + ROPE]
            swapped = jnp.concatenate([tail[:, half:], -tail[:, :half]], axis=1)
            pieces.append(tail * cos2[token] + swapped * sin2[token])
        grad_queries_ref[token, :] = jnp.concatenate(pieces, axis=1).astype(jnp.bfloat16)

    @pl.when(step == pl.num_programs(0) - 1)
    def _():
        for piece, slot in pieces_of:
            grad_keys_ref[slot] = dkey_acc[
                piece * quarter : (piece + 1) * quarter, :width
            ].astype(grad_keys_ref.dtype)


def attention(keys, queries, grad_out, key_up, value_up, cos2, sin2, groups):
    tokens = queries.shape[0]
    half_rows = tokens // 2
    head_count = key_up.shape[1] // NOPE
    group = group_size(head_count)
    key_total = tokens * groups
    key_block = 256
    blocks = key_total // key_block
    padded = LAT + 2 * ROPE
    rows = group * half_rows
    body = functools.partial(
        attention_kernel, groups, group, key_block, (NOPE + ROPE) ** (-0.5)
    )
    whole = lambda shape: pl.BlockSpec(shape, lambda i: (0,) * len(shape), pipeline_mode=pl.Buffered(1))
    column = lambda height, width: pl.BlockSpec((height, group * width), lambda i: (0, i))
    return pl.pallas_call(
        body,
        grid=(head_count // group,),
        in_specs=[
            whole(keys.shape),
            column(tokens, NOPE + ROPE),
            column(tokens, VDIM),
            column(LAT, NOPE),
            column(LAT, VDIM),
            whole(cos2.shape),
            whole(sin2.shape),
        ],
        out_specs=[
            column(tokens, VDIM),
            column(tokens, NOPE + ROPE),
            whole(keys.shape),
        ],
        out_shape=[
            jax.ShapeDtypeStruct((tokens, head_count * VDIM), jnp.bfloat16),
            jax.ShapeDtypeStruct((tokens, head_count * (NOPE + ROPE)), jnp.bfloat16),
            jax.ShapeDtypeStruct(keys.shape, jnp.bfloat16),
        ],
        scratch_shapes=[
            pltpu.VMEM((key_total, padded), jnp.bfloat16),
            pltpu.VMEM((blocks, padded, key_block), jnp.bfloat16),
            pltpu.VMEM((2, rows, padded), jnp.bfloat16),
            pltpu.VMEM((2, rows, LAT), jnp.bfloat16),
            pltpu.VMEM((blocks, rows, key_block), jnp.float32),
            pltpu.VMEM((blocks, rows, key_block), jnp.float32),
            pltpu.VMEM((rows, LAT), jnp.float32),
            pltpu.VMEM((rows, padded), jnp.float32),
            pltpu.VMEM((key_total, padded), jnp.float32),
        ],
        compiler_params=pltpu.CompilerParams(
            dimension_semantics=("arbitrary",), vmem_limit_bytes=60 * 1024 * 1024
        ),
        name="attention",
    )(keys, queries, grad_out, key_up, value_up, cos2, sin2)


class Place:
    def __init__(self):
        index = lax.axis_index("ctx")
        self.core = index % 2
        self.x = (index // 2) % 2
        self.z = index // 4
        self.y = lax.axis_index("tp")
        self.depth = lax.axis_size("ctx") // 4

    def device(self, z=None, x=None, core=None, y=None):
        z = self.z if z is None else z
        x = self.x if x is None else x
        core = self.core if core is None else core
        y = self.y if y is None else y
        return ((z * 2 + x) * 2 + core, y)

    def partners(self):
        others = [
            self.device(z=(self.z + k) % self.depth) for k in range(1, self.depth)
        ]
        sides = [
            self.device(x=1 - self.x),
            self.device(y=1 - self.y),
            self.device(core=1 - self.core),
        ]
        return others, sides

    def greet(self):
        others, sides = self.partners()
        barrier = pltpu.get_barrier_semaphore()
        for device in others + sides:
            pl.semaphore_signal(
                barrier, inc=1, device_id=device, device_id_type=pl.DeviceIdType.MESH
            )
        pl.semaphore_wait(barrier, len(others + sides))


def sender(send_sem, recv_sem):
    def send(slot, source, target, device):
        copy = pltpu.make_async_remote_copy(
            src_ref=source,
            dst_ref=target,
            send_sem=send_sem.at[slot],
            recv_sem=recv_sem.at[slot],
            device_id=device,
            device_id_type=pl.DeviceIdType.MESH,
        )
        copy.start()
        return copy

    return send


def gather_kernel(own_ref, full_ref, send_sem, recv_sem):
    me = Place()
    c, x, y, z = me.core, me.x, me.y, me.z
    others, (across_x, across_y, sibling) = me.partners()
    me.greet()
    send = sender(send_sem, recv_sem)
    base = len(others)
    along = [
        send(k, own_ref, full_ref.at[:, c, y, x, z], device) for k, device in enumerate(others)
    ]
    full_ref[:, c, y, x, z] = own_ref[...]
    for copy in along:
        copy.wait_recv()
    line = full_ref.at[:, c, y, x]
    a2 = send(base, full_ref.at[0, c, y, x], full_ref.at[0, c, y, x], across_x)
    b2 = send(base + 1, full_ref.at[1, c, y, x], full_ref.at[1, c, y, x], across_y)
    c1 = send(base + 2, line, line, sibling)
    a2.wait_recv()
    a3 = send(base + 3, full_ref.at[0, c, y], full_ref.at[0, c, y], across_y)
    got = full_ref.at[0, c, y, 1 - x]
    c2 = send(base + 4, got, got, sibling)
    b2.wait_recv()
    b3 = send(base + 5, full_ref.at[1, c, :, x], full_ref.at[1, c, :, x], across_x)
    got = full_ref.at[1, c, 1 - y, x]
    c3 = send(base + 6, got, got, sibling)
    a3.wait_recv()
    got = full_ref.at[0, c, 1 - y]
    c4 = send(base + 7, got, got, sibling)
    b3.wait_recv()
    got = full_ref.at[1, c, :, 1 - x]
    c5 = send(base + 8, got, got, sibling)
    for copy in (c1, c2, c3, c4, c5):
        copy.wait_recv()
    for copy in along + [a2, b2, c1, a3, c2, b3, c3, c4, c5]:
        copy.wait_send()


def scatter_kernel(
    part_ref, out_ref, got1, sum1, got2, sum2, got3, sum3, got4, send_sem, recv_sem
):
    me = Place()
    c, x, y, z = me.core, me.x, me.y, me.z
    others, (across_x, across_y, sibling) = me.partners()
    me.greet()
    send = sender(send_sem, recv_sem)
    wide = lambda value: value.astype(jnp.float32)
    add = lambda a, b: (wide(a) + wide(b)).astype(jnp.bfloat16)
    base = len(others)
    s0 = send(base, part_ref.at[0, 1 - c, 1 - y], got1.at[0, 1 - y], sibling)
    s1 = send(base + 1, part_ref.at[1, 1 - c, :, 1 - x], got1.at[1, :, 1 - x], sibling)
    s2 = send(base + 2, part_ref.at[0, 1 - c, y], got1.at[0, y], sibling)
    s3 = send(base + 3, part_ref.at[1, 1 - c, :, x], got1.at[1, :, x], sibling)
    s0.wait_recv()
    sum1[0, 1 - y] = add(part_ref[0, c, 1 - y], got1[0, 1 - y])
    a2 = send(base + 4, sum1.at[0, 1 - y], got2.at[0], across_y)
    s1.wait_recv()
    sum1[1, :, 1 - x] = add(part_ref[1, c, :, 1 - x], got1[1, :, 1 - x])
    b2 = send(base + 5, sum1.at[1, :, 1 - x], got2.at[1], across_x)
    s2.wait_recv()
    sum1[0, y] = add(part_ref[0, c, y], got1[0, y])
    s3.wait_recv()
    sum1[1, :, x] = add(part_ref[1, c, :, x], got1[1, :, x])
    a2.wait_recv()
    sum2[0, 1 - x] = add(sum1[0, y, 1 - x], got2[0, 1 - x])
    a3 = send(base + 6, sum2.at[0, 1 - x], got3.at[0], across_x)
    b2.wait_recv()
    sum2[1, 1 - y] = add(sum1[1, 1 - y, x], got2[1, 1 - y])
    b3 = send(base + 7, sum2.at[1, 1 - y], got3.at[1], across_y)
    sum2[0, x] = add(sum1[0, y, x], got2[0, x])
    sum2[1, y] = add(sum1[1, y, x], got2[1, y])
    a3.wait_recv()
    sum3[0] = add(sum2[0, x], got3[0])
    b3.wait_recv()
    sum3[1] = add(sum2[1, y], got3[1])
    along = [
        send(k, sum3.at[:, (z + k + 1) % me.depth], got4.at[k], device)
        for k, device in enumerate(others)
    ]
    total = wide(sum3[:, z])
    for k, copy in enumerate(along):
        copy.wait_recv()
        total = total + wide(got4[k])
    out_ref[...] = total
    for copy in along + [s0, s1, s2, s3, a2, b2, a3, b3]:
        copy.wait_send()


def vmem_call(body, out_shape, scratch, identity, name):
    return pl.pallas_call(
        body,
        out_shape=out_shape,
        in_specs=[pl.BlockSpec(memory_space=pltpu.VMEM)],
        out_specs=pl.BlockSpec(memory_space=pltpu.VMEM),
        scratch_shapes=scratch,
        compiler_params=pltpu.CompilerParams(
            collective_id=identity, has_side_effects=True, vmem_limit_bytes=40 * 1024 * 1024
        ),
        name=name,
    )


def gather_keys(own):
    depth = lax.axis_size("ctx") // 4
    shape = (2, 2, 2, 2, depth) + own.shape[1:]
    sems = pltpu.SemaphoreType.DMA((depth + 8,))
    return vmem_call(
        gather_kernel, jax.ShapeDtypeStruct(shape, own.dtype), [sems, sems], 0, "gather_keys"
    )(own)


def scatter_keys(parts):
    depth = parts.shape[4]
    block = parts.shape[5:]
    sems = pltpu.SemaphoreType.DMA((depth + 7,))
    buffer = lambda *lead: pltpu.VMEM(lead + block, parts.dtype)
    scratch = [
        buffer(2, 2, 2, depth),
        buffer(2, 2, 2, depth),
        buffer(2, 2, depth),
        buffer(2, 2, depth),
        buffer(2, depth),
        buffer(2, depth),
        buffer(depth - 1, 2),
        sems,
        sems,
    ]
    return vmem_call(
        scatter_kernel,
        jax.ShapeDtypeStruct((2,) + block, jnp.float32),
        scratch,
        1,
        "scatter_keys",
    )(parts)


SWAP = [(0, 1), (1, 0)]


def on_device(
    hidden,
    embed,
    gain_hidden,
    gain_embed,
    proj_hidden,
    proj_embed,
    gain_latent,
    key_up,
    value_up,
    queries,
    grad_out,
):
    tokens = hidden.shape[0]
    half_rows = tokens // 2
    groups = lax.axis_size("ctx")
    ctx_index = lax.axis_index("ctx")
    edge_rows = jnp.stack([embed[0], embed[half_rows]], axis=0)
    padded = with_halo(edge_rows, (("ctx", 0),), 1)
    after_early = jnp.where(ctx_index == groups - 1, embed[half_rows], padded[3])
    next_embed = jnp.concatenate(
        [embed[1:half_rows], after_early[None], embed[half_rows + 1 :], padded[0][None]], axis=0
    )
    hidden_wide = hidden.astype(jnp.float32)
    next_wide = next_embed.astype(jnp.float32)
    squares = jnp.stack(
        [jnp.sum(hidden_wide * hidden_wide, axis=1), jnp.sum(next_wide * next_wide, axis=1)], axis=1
    )
    scaled_hidden = (hidden_wide * gain_hidden).astype(jnp.bfloat16)
    scaled_next = (next_wide * gain_embed).astype(jnp.bfloat16)
    part_hidden = jnp.dot(scaled_hidden, proj_hidden, preferred_element_type=jnp.float32)
    part_next = jnp.dot(scaled_next, proj_embed, preferred_element_type=jnp.float32)
    positions = local_positions(tokens, ctx_index, groups)
    cos_table, sin_table = rotation(positions)
    paired = lax.axis_size("tp") == 2
    depth = groups // 4
    quarter = half_rows // 2
    if paired:
        tp_index = lax.axis_index("tp")
        half_of = lambda value, k: lax.dynamic_slice_in_dim(value, k * half_rows, half_rows, 0)
        part_hidden, part_next, squares = (
            half_of(v, tp_index) + lax.ppermute(half_of(v, 1 - tp_index), "tp", SWAP)
            for v in (part_hidden, part_next, squares)
        )
        positions = half_of(positions, tp_index)
    else:
        part_hidden, part_next, squares = lax.psum((part_hidden, part_next, squares), "tp")
    key_latent, key_rope, latent, inverse, inv_latent = finish_latent(
        part_hidden, part_next, squares, gain_latent, positions
    )
    keys = jnp.concatenate([key_latent, key_rope], axis=1)
    if paired:
        keys = gather_keys(keys.reshape(2, quarter, LAT + ROPE))
    else:
        keys = lax.all_gather(keys, "ctx", axis=0, tiled=True)
        keys = keys.reshape(depth, 2, 2, 2, 2, quarter, LAT + ROPE)
        keys = keys.transpose(4, 2, 3, 1, 0, 5, 6)
    attended, grad_queries, grad_keys = attention(
        keys,
        queries,
        grad_out,
        key_up,
        value_up,
        jnp.concatenate([cos_table, cos_table], axis=1),
        jnp.concatenate([sin_table, sin_table], axis=1),
        groups,
    )
    if paired:
        grad_keys = scatter_keys(grad_keys).reshape(half_rows, LAT + ROPE)
    else:
        grad_keys = grad_keys.transpose(4, 3, 1, 2, 0, 5, 6).reshape(-1, LAT + ROPE)
        grad_keys = lax.psum_scatter(grad_keys, "ctx", scatter_dimension=0, tiled=True)
        grad_keys = lax.psum(grad_keys.astype(jnp.float32), "tp")
    grad_key_latent, grad_key_rope = grad_keys[:, :LAT], grad_keys[:, LAT:]
    part_grad_hidden, part_grad_next, coefficient = latent_backward(
        grad_key_latent,
        grad_key_rope,
        latent,
        inverse,
        inv_latent,
        gain_latent,
        positions,
        part_hidden,
        part_next,
    )
    if paired:

        def both_halves(value):
            other = lax.ppermute(value, "tp", SWAP)
            early = jnp.where(tp_index == 0, value, other)
            late = jnp.where(tp_index == 0, other, value)
            return jnp.concatenate([early, late], axis=0)

        part_grad_hidden = both_halves(part_grad_hidden)
        part_grad_next = both_halves(part_grad_next)
        coefficient = both_halves(coefficient)
    grad_hidden = (
        gain_hidden
        * jnp.einsum("rc,dc->rd", part_grad_hidden, proj_hidden, preferred_element_type=jnp.float32)
        - coefficient[:, 0:1] * hidden_wide
    ).astype(jnp.bfloat16)
    grad_next = (
        gain_embed
        * jnp.einsum("rc,dc->rd", part_grad_next, proj_embed, preferred_element_type=jnp.float32)
        - coefficient[:, 1:2] * next_wide
    )
    grad_next_rounded = grad_next.astype(jnp.bfloat16)
    edge_grads = jnp.stack(
        [grad_next_rounded[tokens - 1], grad_next_rounded[half_rows - 1]], axis=0
    )
    returned = with_halo(edge_grads, (("ctx", 0),), 1)
    before_late = jnp.where(ctx_index == groups - 1, grad_next_rounded[half_rows - 1], returned[3])
    grad_embed = jnp.concatenate(
        [
            returned[0][None],
            grad_next_rounded[: half_rows - 1],
            before_late[None],
            grad_next_rounded[half_rows : tokens - 1],
        ],
        axis=0,
    )
    return (attended, grad_queries, grad_hidden, grad_embed)


def solution(mesh):
    placed = (
        P("ctx", "tp"),
        P("ctx", "tp"),
        P("tp"),
        P("tp"),
        P("tp", None),
        P("tp", None),
        P(),
        P(None, "tp"),
        P(None, "tp"),
        P("ctx", "tp"),
        P("ctx", "tp"),
    )
    return jax.shard_map(
        on_device,
        mesh=mesh,
        in_specs=placed,
        out_specs=(P("ctx", "tp"), P("ctx", "tp"), P("ctx", "tp"), P("ctx", "tp")),
        check_vma=False,
    )
```

```python
import functools

import jax
import jax.numpy as jnp
from jax import lax
from jax.experimental import pallas as pl
from jax.experimental.pallas import tpu as pltpu
from jax.sharding import PartitionSpec as P

D = 7168
LAT = 512
ROPE = 64
NOPE = 128
VDIM = 128


EPSILON = 1e-06
ROTARY_BASE = 10000.0


def with_halo(x, sides, width):
    for axis, dim in sides:
        size, length = (lax.axis_size(axis), x.shape[dim])
        up = [(i, (i + 1) % size) for i in range(size - 1)]
        down = [(j, i) for i, j in up]
        last = lax.slice_in_dim(x, length - width, length, axis=dim)
        first = lax.slice_in_dim(x, 0, width, axis=dim)
        before = lax.ppermute(last, axis, up)
        after = lax.ppermute(first, axis, down)
        x = jnp.concatenate([before, x, after], axis=dim)
    return x


def rotation(positions):
    pair_count = ROPE // 2
    frequency = ROTARY_BASE ** (-jnp.arange(pair_count, dtype=jnp.float32) / pair_count)
    angles = positions.astype(jnp.float32)[:, None] * frequency[None, :]
    return (jnp.cos(angles), jnp.sin(angles))


def rotate_pairs(values, cos_table, sin_table):
    pair_count = ROPE // 2
    first_half = values[..., :pair_count]
    second_half = values[..., pair_count:]
    return jnp.concatenate(
        [
            first_half * cos_table - second_half * sin_table,
            first_half * sin_table + second_half * cos_table,
        ],
        axis=-1,
    )


def unrotate(values, cos_table, sin_table):
    pair_count = ROPE // 2
    first_half = values[..., :pair_count]
    second_half = values[..., pair_count:]
    return jnp.concatenate(
        [
            first_half * cos_table + second_half * sin_table,
            second_half * cos_table - first_half * sin_table,
        ],
        axis=-1,
    )


def local_positions(tokens, ctx_index, groups):
    half_rows = tokens // 2
    offsets = jnp.arange(tokens, dtype=jnp.int32)
    early_pos = ctx_index * half_rows + offsets
    late_pos = (2 * groups - 1 - ctx_index) * half_rows + offsets - half_rows
    return jnp.where(offsets < half_rows, early_pos, late_pos)


def finish_latent(part_hidden, part_next, squares, gain_latent, positions):
    inverse = lax.rsqrt(squares / D + EPSILON)
    latent = inverse[:, 0:1] * part_hidden + inverse[:, 1:2] * part_next
    leading = latent[:, :LAT]
    inv_latent = lax.rsqrt(jnp.mean(leading * leading, axis=1, keepdims=True) + EPSILON)
    key_latent = (leading * inv_latent * gain_latent).astype(jnp.bfloat16)
    cos_table, sin_table = rotation(positions)
    key_rope = rotate_pairs(latent[:, LAT:], cos_table, sin_table).astype(jnp.bfloat16)
    return (key_latent, key_rope, latent, inverse, inv_latent)


def latent_backward(
    grad_key_latent,
    grad_key_rope,
    latent,
    inverse,
    inv_latent,
    gain_latent,
    positions,
    part_hidden,
    part_next,
):
    cos_table, sin_table = rotation(positions)
    grad_rope = unrotate(grad_key_rope, cos_table, sin_table)
    leading = latent[:, :LAT]
    gained = gain_latent * grad_key_latent
    grad_leading = (
        inv_latent * gained
        - inv_latent**3 * leading * jnp.sum(gained * leading, axis=1, keepdims=True) / LAT
    )
    grad_latent = jnp.concatenate([grad_leading, grad_rope], axis=1)
    part_grad_hidden = (inverse[:, 0:1] * grad_latent).astype(jnp.bfloat16)
    part_grad_next = (inverse[:, 1:2] * grad_latent).astype(jnp.bfloat16)
    inv_sums = jnp.concatenate(
        [
            jnp.sum(grad_latent * part_hidden, axis=1, keepdims=True),
            jnp.sum(grad_latent * part_next, axis=1, keepdims=True),
        ],
        axis=1,
    )
    coefficient = inv_sums * inverse**3 / D
    return (part_grad_hidden, part_grad_next, coefficient)


UNROLL = 3


def group_size(head_count):
    for size in (8, 4, 2, 1):
        if head_count % size == 0:
            return size


def attention_kernel(
    groups,
    group,
    key_block,
    score_scale,
    keys_ref,
    queries_ref,
    grad_out_ref,
    key_up_ref,
    value_up_ref,
    cos_ref,
    sin_ref,
    attended_ref,
    grad_queries_ref,
    grad_keys_ref,
    table,
    table_t,
    query_rows,
    grad_rows,
    score_buf,
    dprob_buf,
    out_acc,
    dquery_acc,
    dkey_acc,
    row_stat,
):
    step = pl.program_id(0)
    ctx_index = lax.axis_index("ctx")
    tokens = queries_ref.shape[0]
    half_rows = tokens // 2
    rows = group * half_rows
    key_total = table.shape[0]
    width = LAT + ROPE
    padded = table.shape[1]
    blocks = key_total // key_block
    quarter = half_rows // 2
    pieces_of = [
        (2 * c + part, (part, d % 2, y, (d // 2) % 2, d // 4))
        for c in range(2 * groups)
        for y, d in [(0, c) if c < groups else (1, 2 * groups - 1 - c)]
        for part in range(2)
    ]

    @pl.when(step == 0)
    def _():
        dkey_acc[...] = jnp.zeros_like(dkey_acc)
        query_rows[...] = jnp.zeros_like(query_rows)
        for piece, slot in pieces_of:
            chunk = keys_ref[slot]
            pad = jnp.zeros((quarter, padded - width), chunk.dtype)
            table[piece * quarter : (piece + 1) * quarter, :] = jnp.concatenate(
                [chunk, pad], axis=1
            )

        @pl.loop(0, blocks)
        def _(j):
            first = pl.multiple_of(j * key_block, key_block)
            table_t[j] = table[pl.ds(first, key_block), :].T

    cos2 = cos_ref[...]
    sin2 = sin_ref[...]
    half = ROPE // 2
    nt = (((1,), (1,)), ((), ()))
    tn = (((0,), (0,)), ((), ()))
    all_queries = queries_ref[...]
    for g in range(group):
        first = g * (NOPE + ROPE)
        nope = all_queries[:, first : first + NOPE]
        rope = all_queries[:, first + NOPE : first + NOPE + ROPE].astype(jnp.float32)
        swapped = jnp.concatenate([-rope[:, half:], rope[:, :half]], axis=1)
        rotated = (rope * cos2 + swapped * sin2).astype(jnp.bfloat16)
        lead = lax.dot_general(
            nope, key_up_ref[:, g * NOPE : (g + 1) * NOPE], nt, preferred_element_type=jnp.float32
        ).astype(jnp.bfloat16)
        grads = lax.dot_general(
            grad_out_ref[:, g * VDIM : (g + 1) * VDIM],
            value_up_ref[:, g * VDIM : (g + 1) * VDIM],
            nt,
            preferred_element_type=jnp.float32,
        ).astype(jnp.bfloat16)
        for h in range(2):
            source = slice(h * half_rows, (h + 1) * half_rows)
            target = slice(g * half_rows, (g + 1) * half_rows)
            query_rows[h, target, :LAT] = lead[source]
            query_rows[h, target, LAT : LAT + ROPE] = rotated[source]
            grad_rows[h, target, :] = grads[source]

    lanes = 128
    spans = key_block // lanes
    early_pos = ctx_index * half_rows
    late_pos = (2 * groups - 1 - ctx_index) * half_rows
    early_count = (early_pos + half_rows + key_block - 1) // key_block
    tiles = blocks + 1
    unroll = UNROLL if tiles % UNROLL == 0 else 1
    row_off = lax.broadcasted_iota(jnp.int32, (rows, lanes), 0) % half_rows
    gap = row_off - lax.broadcasted_iota(jnp.int32, (rows, lanes), 1)

    def locate(tile):
        late = (tile >= early_count).astype(jnp.int32)
        block = tile - late * early_count
        return late, block, pl.multiple_of(block * key_block, key_block)

    def over_tiles(body):
        @pl.loop(0, tiles // unroll)
        def _(trip):
            for k in range(unroll):
                body(trip * unroll + k)

    row_stat[0] = jnp.full(row_stat.shape[1:], -1e30, jnp.float32)
    row_stat[1] = jnp.zeros(row_stat.shape[1:], jnp.float32)
    row_stat[2] = jnp.zeros(row_stat.shape[1:], jnp.float32)
    out_acc[...] = jnp.zeros_like(out_acc)
    dquery_acc[...] = jnp.zeros_like(dquery_acc)

    def score_tile(tile):
        late, block, first = locate(tile)
        shift = first - jnp.where(late == 1, late_pos, early_pos)
        scores = jnp.dot(query_rows[late], table_t[block], preferred_element_type=jnp.float32)
        running = row_stat[0, late]
        for k in range(spans):
            part = scores[:, k * lanes : (k + 1) * lanes]
            part = jnp.where(gap >= shift + k * lanes, part, -1e30)
            score_buf[tile, :, k * lanes : (k + 1) * lanes] = part
            running = jnp.maximum(running, part)
        row_stat[0, late] = running
        dprob_buf[tile] = jnp.dot(
            grad_rows[late], table_t[block, :LAT, :], preferred_element_type=jnp.float32
        )

    over_tiles(score_tile)
    for h in range(2):
        row_stat[0, h] = jnp.broadcast_to(
            jnp.max(row_stat[0, h], axis=1, keepdims=True), (rows, lanes)
        )

    def weight_tile(tile):
        late, block, first = locate(tile)
        row_max = row_stat[0, late]
        weight_sum = row_stat[1, late]
        delta_sum = row_stat[2, late]
        for k in range(spans):
            span = slice(k * lanes, (k + 1) * lanes)
            weights = jnp.exp((score_buf[tile, :, span] - row_max) * score_scale)
            score_buf[tile, :, span] = weights
            weight_sum = weight_sum + weights
            delta_sum = delta_sum + weights * dprob_buf[tile, :, span]
        row_stat[1, late] = weight_sum
        row_stat[2, late] = delta_sum

    over_tiles(weight_tile)
    for h in range(2):
        inv_sum = 1.0 / jnp.sum(row_stat[1, h], axis=1, keepdims=True)
        delta = jnp.sum(row_stat[2, h], axis=1, keepdims=True) * inv_sum
        row_stat[1, h] = jnp.broadcast_to(inv_sum, (rows, lanes))
        row_stat[2, h] = jnp.broadcast_to(delta, (rows, lanes))

    def grad_tile(tile):
        late, block, first = locate(tile)
        inv_sum = row_stat[1, late]
        delta = row_stat[2, late]
        probs = []
        dscores = []
        for k in range(spans):
            span = slice(k * lanes, (k + 1) * lanes)
            prob = (score_buf[tile, :, span] * inv_sum).astype(jnp.bfloat16)
            probs.append(prob)
            dscores.append(
                (
                    prob.astype(jnp.float32) * (dprob_buf[tile, :, span] - delta) * score_scale
                ).astype(jnp.bfloat16)
            )
        prob = jnp.concatenate(probs, axis=1)
        dscore = jnp.concatenate(dscores, axis=1)
        keys = table[pl.ds(first, key_block), :]
        out_acc[late] += jnp.dot(prob, keys[:, :LAT], preferred_element_type=jnp.float32)
        dquery_acc[late] += jnp.dot(dscore, keys, preferred_element_type=jnp.float32)
        dkey_lead = lax.dot_general(
            dscore, query_rows[late, :, :LAT], tn, preferred_element_type=jnp.float32
        ) + lax.dot_general(prob, grad_rows[late], tn, preferred_element_type=jnp.float32)
        dkey_acc[pl.ds(first, key_block), :LAT] += dkey_lead
        dkey_acc[pl.ds(first, key_block), LAT:] += lax.dot_general(
            dscore, query_rows[late, :, LAT:], tn, preferred_element_type=jnp.float32
        )

    over_tiles(grad_tile)
    pieces = []
    for g in range(group):
        part = slice(g * half_rows, (g + 1) * half_rows)
        both = lambda ref, span: jnp.concatenate([ref[0, part, span], ref[1, part, span]], axis=0)
        attended_ref[:, g * VDIM : (g + 1) * VDIM] = jnp.dot(
            both(out_acc, slice(0, LAT)).astype(jnp.bfloat16),
            value_up_ref[:, g * VDIM : (g + 1) * VDIM],
            preferred_element_type=jnp.float32,
        ).astype(jnp.bfloat16)
        pieces.append(
            jnp.dot(
                both(dquery_acc, slice(0, LAT)).astype(jnp.bfloat16),
                key_up_ref[:, g * NOPE : (g + 1) * NOPE],
                preferred_element_type=jnp.float32,
            )
        )
        tail = both(dquery_acc, slice(LAT, LAT + ROPE))
        swapped = jnp.concatenate([tail[:, half:], -tail[:, :half]], axis=1)
        pieces.append(tail * cos2 + swapped * sin2)
    grad_queries_ref[...] = jnp.concatenate(pieces, axis=1).astype(jnp.bfloat16)

    @pl.when(step == pl.num_programs(0) - 1)
    def _():
        for piece, slot in pieces_of:
            grad_keys_ref[slot] = dkey_acc[
                piece * quarter : (piece + 1) * quarter, :width
            ].astype(grad_keys_ref.dtype)


def attention(keys, queries, grad_out, key_up, value_up, cos2, sin2, groups):
    tokens = queries.shape[0]
    half_rows = tokens // 2
    head_count = key_up.shape[1] // NOPE
    group = group_size(head_count)
    key_total = tokens * groups
    key_block = 256
    blocks = key_total // key_block
    padded = LAT + 2 * ROPE
    rows = group * half_rows
    body = functools.partial(
        attention_kernel, groups, group, key_block, (NOPE + ROPE) ** (-0.5)
    )
    whole = lambda shape: pl.BlockSpec(shape, lambda i: (0,) * len(shape), pipeline_mode=pl.Buffered(1))
    column = lambda height, width: pl.BlockSpec((height, group * width), lambda i: (0, i))
    return pl.pallas_call(
        body,
        grid=(head_count // group,),
        in_specs=[
            whole(keys.shape),
            column(tokens, NOPE + ROPE),
            column(tokens, VDIM),
            column(LAT, NOPE),
            column(LAT, VDIM),
            whole(cos2.shape),
            whole(sin2.shape),
        ],
        out_specs=[
            column(tokens, VDIM),
            column(tokens, NOPE + ROPE),
            whole(keys.shape),
        ],
        out_shape=[
            jax.ShapeDtypeStruct((tokens, head_count * VDIM), jnp.bfloat16),
            jax.ShapeDtypeStruct((tokens, head_count * (NOPE + ROPE)), jnp.bfloat16),
            jax.ShapeDtypeStruct(keys.shape, jnp.bfloat16),
        ],
        scratch_shapes=[
            pltpu.VMEM((key_total, padded), jnp.bfloat16),
            pltpu.VMEM((blocks, padded, key_block), jnp.bfloat16),
            pltpu.VMEM((2, rows, padded), jnp.bfloat16),
            pltpu.VMEM((2, rows, LAT), jnp.bfloat16),
            pltpu.VMEM((blocks + 1, rows, key_block), jnp.float32),
            pltpu.VMEM((blocks + 1, rows, key_block), jnp.float32),
            pltpu.VMEM((2, rows, LAT), jnp.float32),
            pltpu.VMEM((2, rows, padded), jnp.float32),
            pltpu.VMEM((key_total, padded), jnp.float32),
            pltpu.VMEM((3, 2, rows, 128), jnp.float32),
        ],
        compiler_params=pltpu.CompilerParams(
            dimension_semantics=("arbitrary",), vmem_limit_bytes=60 * 1024 * 1024
        ),
        name="attention",
    )(keys, queries, grad_out, key_up, value_up, cos2, sin2)


class Place:
    def __init__(self):
        index = lax.axis_index("ctx")
        self.core = index % 2
        self.x = (index // 2) % 2
        self.z = index // 4
        self.y = lax.axis_index("tp")
        self.depth = lax.axis_size("ctx") // 4

    def device(self, z=None, x=None, core=None, y=None):
        z = self.z if z is None else z
        x = self.x if x is None else x
        core = self.core if core is None else core
        y = self.y if y is None else y
        return ((z * 2 + x) * 2 + core, y)

    def partners(self):
        others = [
            self.device(z=(self.z + k) % self.depth) for k in range(1, self.depth)
        ]
        sides = [
            self.device(x=1 - self.x),
            self.device(y=1 - self.y),
            self.device(core=1 - self.core),
        ]
        return others, sides

    def greet(self):
        others, sides = self.partners()
        barrier = pltpu.get_barrier_semaphore()
        for device in others + sides:
            pl.semaphore_signal(
                barrier, inc=1, device_id=device, device_id_type=pl.DeviceIdType.MESH
            )
        pl.semaphore_wait(barrier, len(others + sides))


def sender(send_sem, recv_sem):
    def send(slot, source, target, device):
        copy = pltpu.make_async_remote_copy(
            src_ref=source,
            dst_ref=target,
            send_sem=send_sem.at[slot],
            recv_sem=recv_sem.at[slot],
            device_id=device,
            device_id_type=pl.DeviceIdType.MESH,
        )
        copy.start()
        return copy

    return send


def gather_kernel(own_ref, full_ref, send_sem, recv_sem):
    me = Place()
    c, x, y, z = me.core, me.x, me.y, me.z
    others, (across_x, across_y, sibling) = me.partners()
    me.greet()
    send = sender(send_sem, recv_sem)
    base = len(others)
    along = [
        send(k, own_ref, full_ref.at[:, c, y, x, z], device) for k, device in enumerate(others)
    ]
    full_ref[:, c, y, x, z] = own_ref[...]
    for copy in along:
        copy.wait_recv()
    line = full_ref.at[:, c, y, x]
    a2 = send(base, full_ref.at[0, c, y, x], full_ref.at[0, c, y, x], across_x)
    b2 = send(base + 1, full_ref.at[1, c, y, x], full_ref.at[1, c, y, x], across_y)
    c1 = send(base + 2, line, line, sibling)
    a2.wait_recv()
    a3 = send(base + 3, full_ref.at[0, c, y], full_ref.at[0, c, y], across_y)
    got = full_ref.at[0, c, y, 1 - x]
    c2 = send(base + 4, got, got, sibling)
    b2.wait_recv()
    b3 = send(base + 5, full_ref.at[1, c, :, x], full_ref.at[1, c, :, x], across_x)
    got = full_ref.at[1, c, 1 - y, x]
    c3 = send(base + 6, got, got, sibling)
    a3.wait_recv()
    got = full_ref.at[0, c, 1 - y]
    c4 = send(base + 7, got, got, sibling)
    b3.wait_recv()
    got = full_ref.at[1, c, :, 1 - x]
    c5 = send(base + 8, got, got, sibling)
    for copy in (c1, c2, c3, c4, c5):
        copy.wait_recv()
    for copy in along + [a2, b2, c1, a3, c2, b3, c3, c4, c5]:
        copy.wait_send()


def scatter_kernel(
    part_ref, out_ref, got1, sum1, got2, sum2, got3, sum3, got4, send_sem, recv_sem
):
    me = Place()
    c, x, y, z = me.core, me.x, me.y, me.z
    others, (across_x, across_y, sibling) = me.partners()
    me.greet()
    send = sender(send_sem, recv_sem)
    wide = lambda value: value.astype(jnp.float32)
    add = lambda a, b: (wide(a) + wide(b)).astype(jnp.bfloat16)
    base = len(others)
    s0 = send(base, part_ref.at[0, 1 - c, 1 - y], got1.at[0, 1 - y], sibling)
    s1 = send(base + 1, part_ref.at[1, 1 - c, :, 1 - x], got1.at[1, :, 1 - x], sibling)
    s2 = send(base + 2, part_ref.at[0, 1 - c, y], got1.at[0, y], sibling)
    s3 = send(base + 3, part_ref.at[1, 1 - c, :, x], got1.at[1, :, x], sibling)
    s0.wait_recv()
    sum1[0, 1 - y] = add(part_ref[0, c, 1 - y], got1[0, 1 - y])
    a2 = send(base + 4, sum1.at[0, 1 - y], got2.at[0], across_y)
    s1.wait_recv()
    sum1[1, :, 1 - x] = add(part_ref[1, c, :, 1 - x], got1[1, :, 1 - x])
    b2 = send(base + 5, sum1.at[1, :, 1 - x], got2.at[1], across_x)
    s2.wait_recv()
    sum1[0, y] = add(part_ref[0, c, y], got1[0, y])
    s3.wait_recv()
    sum1[1, :, x] = add(part_ref[1, c, :, x], got1[1, :, x])
    a2.wait_recv()
    sum2[0, 1 - x] = add(sum1[0, y, 1 - x], got2[0, 1 - x])
    a3 = send(base + 6, sum2.at[0, 1 - x], got3.at[0], across_x)
    b2.wait_recv()
    sum2[1, 1 - y] = add(sum1[1, 1 - y, x], got2[1, 1 - y])
    b3 = send(base + 7, sum2.at[1, 1 - y], got3.at[1], across_y)
    sum2[0, x] = add(sum1[0, y, x], got2[0, x])
    sum2[1, y] = add(sum1[1, y, x], got2[1, y])
    a3.wait_recv()
    sum3[0] = add(sum2[0, x], got3[0])
    b3.wait_recv()
    sum3[1] = add(sum2[1, y], got3[1])
    along = [
        send(k, sum3.at[:, (z + k + 1) % me.depth], got4.at[k], device)
        for k, device in enumerate(others)
    ]
    total = wide(sum3[:, z])
    for k, copy in enumerate(along):
        copy.wait_recv()
        total = total + wide(got4[k])
    out_ref[...] = total
    for copy in along + [s0, s1, s2, s3, a2, b2, a3, b3]:
        copy.wait_send()


def vmem_call(body, out_shape, scratch, identity, name):
    return pl.pallas_call(
        body,
        out_shape=out_shape,
        in_specs=[pl.BlockSpec(memory_space=pltpu.VMEM)],
        out_specs=pl.BlockSpec(memory_space=pltpu.VMEM),
        scratch_shapes=scratch,
        compiler_params=pltpu.CompilerParams(
            collective_id=identity, has_side_effects=True, vmem_limit_bytes=40 * 1024 * 1024
        ),
        name=name,
    )


def gather_keys(own):
    depth = lax.axis_size("ctx") // 4
    shape = (2, 2, 2, 2, depth) + own.shape[1:]
    sems = pltpu.SemaphoreType.DMA((depth + 8,))
    return vmem_call(
        gather_kernel, jax.ShapeDtypeStruct(shape, own.dtype), [sems, sems], 0, "gather_keys"
    )(own)


def scatter_keys(parts):
    depth = parts.shape[4]
    block = parts.shape[5:]
    sems = pltpu.SemaphoreType.DMA((depth + 7,))
    buffer = lambda *lead: pltpu.VMEM(lead + block, parts.dtype)
    scratch = [
        buffer(2, 2, 2, depth),
        buffer(2, 2, 2, depth),
        buffer(2, 2, depth),
        buffer(2, 2, depth),
        buffer(2, depth),
        buffer(2, depth),
        buffer(depth - 1, 2),
        sems,
        sems,
    ]
    return vmem_call(
        scatter_kernel,
        jax.ShapeDtypeStruct((2,) + block, jnp.float32),
        scratch,
        1,
        "scatter_keys",
    )(parts)


SWAP = [(0, 1), (1, 0)]


def on_device(
    hidden,
    embed,
    gain_hidden,
    gain_embed,
    proj_hidden,
    proj_embed,
    gain_latent,
    key_up,
    value_up,
    queries,
    grad_out,
):
    tokens = hidden.shape[0]
    half_rows = tokens // 2
    groups = lax.axis_size("ctx")
    ctx_index = lax.axis_index("ctx")
    edge_rows = jnp.stack([embed[0], embed[half_rows]], axis=0)
    padded = with_halo(edge_rows, (("ctx", 0),), 1)
    after_early = jnp.where(ctx_index == groups - 1, embed[half_rows], padded[3])
    next_embed = jnp.concatenate(
        [embed[1:half_rows], after_early[None], embed[half_rows + 1 :], padded[0][None]], axis=0
    )
    hidden_wide = hidden.astype(jnp.float32)
    next_wide = next_embed.astype(jnp.float32)
    squares = jnp.stack(
        [jnp.sum(hidden_wide * hidden_wide, axis=1), jnp.sum(next_wide * next_wide, axis=1)], axis=1
    )
    scaled_hidden = (hidden_wide * gain_hidden).astype(jnp.bfloat16)
    scaled_next = (next_wide * gain_embed).astype(jnp.bfloat16)
    part_hidden = jnp.dot(scaled_hidden, proj_hidden, preferred_element_type=jnp.float32)
    part_next = jnp.dot(scaled_next, proj_embed, preferred_element_type=jnp.float32)
    positions = local_positions(tokens, ctx_index, groups)
    cos_table, sin_table = rotation(positions)
    paired = lax.axis_size("tp") == 2
    depth = groups // 4
    quarter = half_rows // 2
    if paired:
        tp_index = lax.axis_index("tp")
        half_of = lambda value, k: lax.dynamic_slice_in_dim(value, k * half_rows, half_rows, 0)
        part_hidden, part_next, squares = (
            half_of(v, tp_index) + lax.ppermute(half_of(v, 1 - tp_index), "tp", SWAP)
            for v in (part_hidden, part_next, squares)
        )
        positions = half_of(positions, tp_index)
    else:
        part_hidden, part_next, squares = lax.psum((part_hidden, part_next, squares), "tp")
    key_latent, key_rope, latent, inverse, inv_latent = finish_latent(
        part_hidden, part_next, squares, gain_latent, positions
    )
    keys = jnp.concatenate([key_latent, key_rope], axis=1)
    if paired:
        keys = gather_keys(keys.reshape(2, quarter, LAT + ROPE))
    else:
        keys = lax.all_gather(keys, "ctx", axis=0, tiled=True)
        keys = keys.reshape(depth, 2, 2, 2, 2, quarter, LAT + ROPE)
        keys = keys.transpose(4, 2, 3, 1, 0, 5, 6)
    attended, grad_queries, grad_keys = attention(
        keys,
        queries,
        grad_out,
        key_up,
        value_up,
        jnp.concatenate([cos_table, cos_table], axis=1),
        jnp.concatenate([sin_table, sin_table], axis=1),
        groups,
    )
    if paired:
        grad_keys = scatter_keys(grad_keys).reshape(half_rows, LAT + ROPE)
    else:
        grad_keys = grad_keys.transpose(4, 3, 1, 2, 0, 5, 6).reshape(-1, LAT + ROPE)
        grad_keys = lax.psum_scatter(grad_keys, "ctx", scatter_dimension=0, tiled=True)
        grad_keys = lax.psum(grad_keys.astype(jnp.float32), "tp")
    grad_key_latent, grad_key_rope = grad_keys[:, :LAT], grad_keys[:, LAT:]
    part_grad_hidden, part_grad_next, coefficient = latent_backward(
        grad_key_latent,
        grad_key_rope,
        latent,
        inverse,
        inv_latent,
        gain_latent,
        positions,
        part_hidden,
        part_next,
    )
    if paired:

        def both_halves(value):
            other = lax.ppermute(value, "tp", SWAP)
            early = jnp.where(tp_index == 0, value, other)
            late = jnp.where(tp_index == 0, other, value)
            return jnp.concatenate([early, late], axis=0)

        part_grad_hidden = both_halves(part_grad_hidden)
        part_grad_next = both_halves(part_grad_next)
        coefficient = both_halves(coefficient)
    grad_hidden = (
        gain_hidden
        * jnp.einsum("rc,dc->rd", part_grad_hidden, proj_hidden, preferred_element_type=jnp.float32)
        - coefficient[:, 0:1] * hidden_wide
    ).astype(jnp.bfloat16)
    grad_next = (
        gain_embed
        * jnp.einsum("rc,dc->rd", part_grad_next, proj_embed, preferred_element_type=jnp.float32)
        - coefficient[:, 1:2] * next_wide
    )
    grad_next_rounded = grad_next.astype(jnp.bfloat16)
    edge_grads = jnp.stack(
        [grad_next_rounded[tokens - 1], grad_next_rounded[half_rows - 1]], axis=0
    )
    returned = with_halo(edge_grads, (("ctx", 0),), 1)
    before_late = jnp.where(ctx_index == groups - 1, grad_next_rounded[half_rows - 1], returned[3])
    grad_embed = jnp.concatenate(
        [
            returned[0][None],
            grad_next_rounded[: half_rows - 1],
            before_late[None],
            grad_next_rounded[half_rows : tokens - 1],
        ],
        axis=0,
    )
    return (attended, grad_queries, grad_hidden, grad_embed)


def solution(mesh):
    placed = (
        P("ctx", "tp"),
        P("ctx", "tp"),
        P("tp"),
        P("tp"),
        P("tp", None),
        P("tp", None),
        P(),
        P(None, "tp"),
        P(None, "tp"),
        P("ctx", "tp"),
        P("ctx", "tp"),
    )
    return jax.shard_map(
        on_device,
        mesh=mesh,
        in_specs=placed,
        out_specs=(P("ctx", "tp"), P("ctx", "tp"), P("ctx", "tp"), P("ctx", "tp")),
        check_vma=False,
    )
```
